32 devices in a mesh: tm: 8 (over z, core), space: 4 (over y, x).
Axes of the slice: x: 2, y: 2, z: 4, core: 2. Of those that a mesh axis runs over, the one named last changes fastest.
Arguments:
- initial_temp: float32 [64, 32, 256], P('space'), may hold values from -6 to 6
- region_labels: int32 [16, 8, 64], P('space'), may hold values from 0 to 5
- region_rate: float32 [6], replicated, may hold values from 0.5 to 8
- heat_rate: float32 [8, 6], replicated, may hold values from 0.1 to 2
Outputs:
- slice_end: float32 [8, 64, 32, 256], P('tm', 'space')
The draws below stay inside these ranges and needn't reach their ends.
All inputs are finite; a program needn't handle non-finite values.
Results may differ from the reference program's by a relative error of at most 0.0001.
Values sent between devices are 32-bit elements; how exact they have to be, the bound alone decides.
A program may use at most 128 MiB of HBM per device.

```python
import math
import jax
import jax.numpy as jnp
from jax import lax

NY = 32
NZ = 256
FINE_STEPS = 2
SWEEPS = 8
C_SWEEPS = 4
PARA_ITERS = 2
REGIONS = 6
SLICES = 8
NX = 64


def with_ends(drawn, key, least, top_value):
    longest = drawn.shape.index(max(drawn.shape))
    spots = []
    for shift in (0, 1):
        where = [jax.random.randint(jax.random.fold_in(key, axis), (), 0, length) for axis, length in enumerate(drawn.shape)]
        where[longest] = (where[longest] + shift) % drawn.shape[longest]
        spots.append(tuple(where))
    return drawn.at[spots[0]].set(least).at[spots[1]].set(top_value)


def level_of(stream_key, extent, cuts, smallest, top_value):
    factor_of = 1.0
    for axis_at, shards_of in cuts:
        steps = jax.random.uniform(jax.random.fold_in(jax.random.fold_in(stream_key, 6), axis_at), (shards_of,), jnp.float32, smallest / len(cuts), top_value / len(cuts))
        factor_of = factor_of * jnp.repeat(jnp.exp(steps), extent[axis_at] // shards_of).reshape((-1,) + (1,) * (len(extent) - 1 - axis_at))
    return factor_of


def scatter_about(stream_key, shape, width, reach, shards=(), held_as=jnp.bfloat16):
    gain = level_of(stream_key, shape, shards, -0.22, 0.18) if shards else 1.0
    drawn = jax.random.normal(stream_key, shape, jnp.float32) * width * gain
    return jnp.minimum(jnp.maximum(drawn, -reach), reach).astype(held_as)


def setup_inputs(seed: int = 0) -> dict:
    seeds = jax.random.split(jax.random.key(seed), 5)
    return {
        "initial_temp": scatter_about(seeds[0], (NX, NY, NZ), 1.0, 6.0, ((0, 4),), jnp.float32),
        "region_labels": with_ends(jax.random.randint(seeds[1], (NX // 4, NY // 4, NZ // 4), 0, REGIONS), jax.random.fold_in(seeds[1], 1), 0, REGIONS - 1).astype(jnp.int32),
        "region_rate": jnp.clip(jnp.exp(jax.random.uniform(seeds[2], (REGIONS,), jnp.float32, math.log(0.5), math.log(8.0))), 0.5, 8.0),
        "heat_rate": jnp.clip(jax.random.uniform(seeds[3], (SLICES, REGIONS), jnp.float32, 0.1, 2.0), 0.1, 2.0),
    }


def neighbours(field):
    padded = jnp.pad(field, 1)
    total = padded[2:, 1:-1, 1:-1] + padded[:-2, 1:-1, 1:-1]
    total = total + padded[1:-1, 2:, 1:-1] + padded[1:-1, :-2, 1:-1]
    total = total + padded[1:-1, 1:-1, 2:] + padded[1:-1, 1:-1, :-2]
    return total


def expand(block):
    lead = block.shape[:-3]
    sx, sy, sz = block.shape[-3:]
    wide = jnp.broadcast_to(block[..., :, None, :, None, :, None], lead + (sx, 4, sy, 4, sz, 4))
    return wide.reshape(lead + (4 * sx, 4 * sy, 4 * sz))


def restrict(field):
    lead = field.shape[:-3]
    sx, sy, sz = field.shape[-3:]
    split = field.reshape(lead + (sx // 4, 4, sy // 4, 4, sz // 4, 4))
    return jnp.mean(split, axis=(-5, -3, -1))


def propagate(state, inverse, weight, source, count, sweeps):
    for outer_index in range(count):
        scaled = (state + source) * inverse
        field = state
        for sweep_index in range(sweeps):
            field = scaled + weight * neighbours(field)
        state = field
    return state


def reference(initial_temp, region_labels, region_rate, heat_rate):
    rate = region_rate[region_labels]
    rate_fine = expand(rate)
    inv_fine = 1.0 / (1.0 + 6.0 * rate_fine)
    weight_fine = rate_fine * inv_fine
    rate_coarse = FINE_STEPS * rate / 16.0
    inv_coarse = 1.0 / (1.0 + 6.0 * rate_coarse)
    weight_coarse = rate_coarse * inv_coarse

    def fine_one(state, row):
        return propagate(state, inv_fine, weight_fine, expand(row[region_labels]), FINE_STEPS, SWEEPS)

    def coarse_one(coarse, row):
        return propagate(coarse, inv_coarse, weight_coarse, FINE_STEPS * row[region_labels], 1, C_SWEEPS)

    start = restrict(initial_temp)

    def chain(deltas):
        def advance(coarse, pair):
            row, delta = pair
            return coarse_one(coarse, row) + delta, coarse

        unused, starts = lax.scan(advance, start, (heat_rate, deltas))
        return starts, jax.vmap(coarse_one)(starts, heat_rate)

    starts, ends = chain(jnp.zeros((SLICES,) + start.shape, jnp.float32))
    states = jnp.concatenate([initial_temp[None], expand(starts[1:])], axis=0)
    corrected = states
    for iteration in range(PARA_ITERS):
        fine_ends = jax.vmap(fine_one)(states, heat_rate)
        starts, new_ends = chain(restrict(fine_ends) - ends)
        corrected = fine_ends + expand(new_ends - ends)
        ends = new_ends
        states = jnp.concatenate([initial_temp[None], corrected[:-1]], axis=0)
    return corrected
```

```python
import functools

import jax
import jax.numpy as jnp
from jax import lax
from jax.experimental import pallas as pl
from jax.experimental.pallas import tpu as pltpu
from jax.sharding import PartitionSpec as P

FINE_STEPS = 2
SWEEPS = 8
C_SWEEPS = 4
W = FINE_STEPS * SWEEPS
COARSE = 4
F32 = jnp.float32
BF16 = jnp.bfloat16
MESH = pl.DeviceIdType.MESH
HI = lax.Precision.HIGHEST
UNROLL = 4
WIDE = 8

ROW = (16, 0, 8, 32)
ROWS = 40


def kernel(
    n_count, s_count,
    init_hbm, labels_hbm, rates_hbm, heat_hbm,
    out,
    raw, labels, rates, heat, in_sem,
    init, nbr, ag, m1, m2, cst, w1, dl, clin, llin, wtp, inv, src, u, v, sc,
    ag_ss, ag_rs, i_ss, i_rs, m1_ss, m1_rs, m2_ss, m2_rs,
):
    n = lax.axis_index("tm")
    s = lax.axis_index("space")
    planes, ny, nz = init_hbm.shape
    bx, cy, cz = labels_hbm.shape
    cx = bx * s_count
    cq = cx // 2
    lanes = 2 * cz
    zs = nz // lanes
    regions = rates_hbm.shape[1]
    half = planes // 2
    bh = bx // 2
    pad = 2 * W // COARSE
    inner = W + half
    outer = W
    every = outer + inner
    has_prev = n > 0

    pairs = [(labels_hbm, labels), (rates_hbm, rates), (heat_hbm, heat)]
    pairs += [(init_hbm.at[:, :, pl.ds(c * lanes, lanes)], raw.at[c]) for c in range(zs)]
    fetches = [pltpu.make_async_copy(a, b, in_sem.at[i]) for i, (a, b) in enumerate(pairs)]
    for fetch in fetches:
        fetch.start()

    total = n_count * s_count
    barrier = pltpu.get_barrier_semaphore()

    def greet(k, _):
        other = lax.rem(n * s_count + s + k, total)
        pl.semaphore_signal(
            barrier, inc=1, device_id=(other // s_count, lax.rem(other, s_count)), device_id_type=MESH)
        return 0
    lax.fori_loop(1, total, greet, 0)

    def remote(a, b, ss, rs, dev):
        return pltpu.make_async_remote_copy(
            src_ref=a, dst_ref=b, send_sem=ss, recv_sem=rs, device_id=dev, device_id_type=MESH)

    lane = lax.broadcasted_iota(jnp.int32, (cy, lanes), 1)
    h0 = lane < cz
    z_first, z_last = lane % cz == 0, lane % cz == cz - 1
    zero = jnp.zeros((cy, lanes), F32)

    def swap(x):
        return pltpu.roll(x, cz, x.ndim - 1)

    def rows(t):
        return slice(ROW[t], ROW[t] + cy)

    def packed(t):
        return slice(t * cy, (t + 1) * cy)

    def clear_v(i, _):
        for k in range(outer + 2):
            for c in range(4):
                v[i, k, c, 24:32] = zero
        return 0
    lax.fori_loop(0, W + 1, clear_v, 0)

    def clear_u(k, _):
        for i in range(2):
            for c in range(4):
                u[i, k, c, 24:32] = zero
        return 0
    lax.fori_loop(0, inner + 2, clear_u, 0)
    for i in range(2):
        for c in range(4):
            for t in range(4):
                u[i, 0, c, rows(t)] = zero
    for k in range(pad):
        for at in (k, pad + cx + k):
            clin[at] = zero
            llin[at] = zero - 1.0

    zi = lax.broadcasted_iota(jnp.int32, (nz, nz), 0)
    zj = lax.broadcasted_iota(jnp.int32, (nz, nz), 1)
    to_tiles = jnp.where(zi == 4 * (zj % cz) + zj // cz, F32(1.0), F32(0.0)).astype(BF16)
    from_tiles = jnp.where(zj == 4 * (zi % cz) + zi // cz, F32(1.0), F32(0.0)).astype(BF16)

    def permute(x, one_hot):
        high = x.astype(BF16)
        rest = x - high.astype(F32)
        middle = rest.astype(BF16)
        low = (rest - middle.astype(F32)).astype(BF16)
        parts = [jnp.dot(y, one_hot, preferred_element_type=F32) for y in (high, middle, low)]
        return (parts[0] + parts[1]) + parts[2]

    for fetch in fetches:
        fetch.wait()

    def load(q, _):
        x = jnp.concatenate([
            jnp.concatenate([raw[c, plane, pl.ds(t, cy, stride=4), :] for c in range(zs)], 1)
            for r in range(2) for plane in (2 * q + r, planes - 1 - 2 * q - r) for t in range(4)], 0)
        moved = permute(x, to_tiles)
        for r in range(2):
            for t in range(4):
                for e in range(zs):
                    a = (r * 8 + t) * cy
                    b = (r * 8 + 4 + t) * cy
                    ta = moved[a:a + cy, e * lanes:(e + 1) * lanes]
                    tb = moved[b:b + cy, e * lanes:(e + 1) * lanes]
                    init[2 * q + r, 2 * e, packed(t)] = jnp.where(h0, ta, swap(tb))
                    init[2 * q + r, 2 * e + 1, packed(t)] = jnp.where(h0, swap(ta), tb)
        return 0
    lax.fori_loop(0, half // 2, load, 0)

    def restrict(tile):
        sums = []
        for q in range(bh):
            parts = [tile(COARSE * q + r, c, t) for r in range(COARSE) for c in range(4) for t in range(4)]
            while len(parts) > 1:
                parts = [a + b for a, b in zip(parts[::2], parts[1::2])]
            sums.append(parts[0] * F32(1.0 / 64.0))
        return sums

    li = lax.broadcasted_iota(jnp.int32, (cz, lanes), 0)
    lj = lax.broadcasted_iota(jnp.int32, (cz, lanes), 1)
    spread = [jnp.where(li == lj - h * cz, F32(1.0), F32(0.0)) for h in range(2)]
    means = restrict(lambda p, c, t: init[p, c, packed(t)])
    for q in range(bh):
        ag[s, q] = means[q]
        near = labels[q].astype(F32)
        far = labels[bx - 1 - q].astype(F32)
        ag[s, bh + q] = (jnp.dot(near, spread[0], precision=HI, preferred_element_type=F32)
                         + jnp.dot(far, spread[1], precision=HI, preferred_element_type=F32))

    pl.semaphore_wait(barrier, total - 1)

    gather = []
    for j in range(1, s_count):
        copy = remote(ag.at[s], ag.at[s], ag_ss.at[j], ag_rs.at[j], (n, lax.rem(s + j, s_count)))
        copy.start()
        gather.append(copy)

    aside = min(3, n_count - 1)
    has_lo, has_hi = s > 0, s < s_count - 1

    def to_even(c):
        return c & (lax.rem(s, 2) == 0)

    def to_odd(c):
        return c & (lax.rem(s, 2) == 1)
    routes = [
        (0, 1, 2, (n == 0) & (s < s_count - 2)),
        (3, 1, -2, (n == 0) & (s > 1)),
        (1, 0, 1, to_even((n == 1) & has_hi)),
        (2, 0, -1, to_odd((n == 1) & has_lo)),
        (1, 1 - aside, 1, to_odd((n == aside) & has_hi)),
        (2, 1 - aside, -1, to_even((n == aside) & has_lo)),
    ]
    spreads = [(cond, remote(init, nbr.at[slot], i_ss.at[k], i_rs.at[slot], (n + dn, s + ds)))
               for k, (slot, dn, ds, cond) in enumerate(routes)]
    for cond, copy in spreads:
        @pl.when(cond)
        def _(copy=copy):
            copy.start()
    there = [s > 1, has_lo, has_hi, s < s_count - 2]
    passed = [remote(nbr.at[slot], nbr.at[slot], i_ss.at[6 + k], i_rs.at[slot], (n - 1, s))
              for k, slot in enumerate((1, 2))]

    for slot in range(4):
        @pl.when((n <= 1) & jnp.logical_not(there[slot]))
        def _(slot=slot):
            def wipe(p, _):
                for c in range(4):
                    for t in range(4):
                        nbr[slot, p, c, packed(t)] = zero
                return 0
            lax.fori_loop(0, half, wipe, 0)

    for copy in gather:
        copy.wait()

    def spread_out(block):
        parts = []
        for q in range(cq):
            b, r = q // bx, q % bx
            if r < bh:
                parts.append(jnp.where(h0, block(b, r), block(s_count - 1 - b, r)))
            else:
                at = bx - 1 - r
                parts.append(swap(jnp.where(h0, block(s_count - 1 - b, at), block(b, at))))
        return jnp.stack(parts, 0)

    def to_line(ref, g):
        for q in range(cq):
            x, y = g[q], swap(g[q])
            ref[pad + q] = jnp.where(h0, x, y)
            ref[pad + cx - 1 - q] = jnp.where(h0, y, x)

    def local(ref, q):
        return jnp.where(h0, ref[bx * s + q], ref[bx * s + bx + 2 * pad - 1 - q])

    def lookup(lab, row):
        value = jnp.zeros(lab.shape, F32)
        for r in range(regions):
            value = value + jnp.where(lab == F32(r), row(r), F32(0.0))
        return value

    crow = lax.broadcasted_iota(jnp.int32, (cq, cy, lanes), 1)
    ccol = lax.broadcasted_iota(jnp.int32, (cq, cy, lanes), 2)
    c_first, c_last = crow == 0, crow == cy - 1
    cz_first, cz_last = ccol % cz == 0, ccol % cz == cz - 1
    czero = jnp.zeros((1, cy, lanes), F32)

    def c_neighbours(x):
        value = (jnp.concatenate([czero, x[:-1]], 0)
                 + jnp.concatenate([x[1:], swap(x[-1:])], 0))
        value = value + (jnp.where(c_first, F32(0.0), pltpu.roll(x, 1, 1))
                         + jnp.where(c_last, F32(0.0), pltpu.roll(x, cy - 1, 1)))
        return value + (jnp.where(cz_first, F32(0.0), pltpu.roll(x, 1, 2))
                        + jnp.where(cz_last, F32(0.0), pltpu.roll(x, lanes - 1, 2)))

    lab_all = spread_out(lambda b, r: ag[b, bh + r])
    c_rate = FINE_STEPS * lookup(lab_all, lambda r: rates[0, r]) / 16.0
    c_inv = 1.0 / (1.0 + 6.0 * c_rate)
    c_weight = c_rate * c_inv

    def c_jacobi(scaled, x):
        for _ in range(C_SWEEPS):
            x = scaled + c_weight * c_neighbours(x)
        return x

    cst[0] = spread_out(lambda b, r: ag[b, r])

    def advance(m, c):
        source = FINE_STEPS * lookup(lab_all, lambda r: heat[m, r])
        c = c_jacobi((c + source) * c_inv, c)
        cst[m + 1] = c
        return c

    to_line(llin, lab_all)

    @pl.when(n > 1)
    def _():
        to_line(clin, lax.fori_loop(0, n - 1, advance, cst[0]))
    slice_of_a = n - jnp.where(has_prev, 1, 0).astype(jnp.int32)

    for q in range(every // COARSE):
        lab = local(llin, q)
        rate = lookup(lab, lambda r: rates[0, r])
        iv = 1.0 / (1.0 + 6.0 * rate)
        inv[q] = iv
        src[q] = lookup(lab, lambda r: heat[slice_of_a, r])
        for r in range(COARSE):
            wtp[COARSE * q + r] = rate * iv

    def update(ref, level, k, p, step, put):
        def get(at, t, c):
            return ref[level, at, c, rows(t)]
        below, here, above = k, k + 1, k + 2
        g = [[ref[level, here, c, ROW[3] - 1:ROW[3] - 1 + cy] for c in range(4)]]
        g += [[get(here, t, c) for c in range(4)] for t in range(4)]
        g += [[ref[level, here, c, ROW[0] + 1:ROW[0] + 1 + cy] for c in range(4)]]
        for t in range(4):
            g[t + 1].append(jnp.where(z_last, F32(0.0), pltpu.roll(g[t + 1][0], lanes - 1, 1)))
        d = [[g[a + 1][b + 1] + g[a + 2][b] if a >= 0 or b < 3 else None for b in range(4)] for a in range(-1, 4)]
        left = [g[a + 1][0] + jnp.where(z_first, F32(0.0), pltpu.roll(g[a + 2][3], 1, 1)) for a in range(-1, 3)]
        we = wtp[p]
        for t in range(4):
            for c in range(4):
                around = d[t + 1][c] + (left[t] if c == 0 else d[t][c - 1])
                around = around + (get(below, t, c) + get(above, t, c))
                put(c, t, sc[step, p, c, packed(t)] + we * around)

    def scale(step, first, p0, count, plane):
        def quad(q, _):
            iv, so = inv[p0 // COARSE + q], src[p0 // COARSE + q]
            for r in range(COARSE):
                for c in range(4):
                    for t in range(4):
                        sc[step, p0 + COARSE * q + r, c, packed(t)] = (plane(COARSE * q + r, c, t) + so) * iv
            return 0
        lax.fori_loop(first, count // COARSE, quad, 0)

    quads = inner // UNROLL

    def solve_inner():
        def fine_step(step, _):
            scale(step, SWEEPS // COARSE * step, outer, inner, lambda p, c, t: u[0, 1 + p, c, rows(t)])

            def sweep(i, now):
                then = 1 - now

                def quad(q, edge):
                    for r in range(UNROLL):
                        p = UNROLL * q + r

                        def put(c, t, value, p=p, r=r):
                            u[then, 1 + p, c, rows(t)] = value
                            if edge and r == UNROLL - 1:
                                u[then, 2 + p, c, rows(t)] = swap(value)
                        update(u, now, p, outer + p, step, put)
                    return 0
                lax.fori_loop((1 + i) // UNROLL, quads - 1, lambda q, _: quad(q, False), 0)
                quad(quads - 1, True)
                for e in range(2):
                    for c in range(4):
                        for t in range(4):
                            v[i + 1, outer + e, c, rows(t)] = u[then, 2 + i + e, c, rows(t)]

            def two(j, _):
                sweep(SWEEPS * step + 2 * j, 0)
                sweep(SWEEPS * step + 2 * j + 1, 1)
                return 0
            lax.fori_loop(0, SWEEPS // 2, two, 0)
            return 0
        lax.fori_loop(0, FINE_STEPS, fine_step, 0)

    def solve_outer():
        def fine_step(step, _):
            p0 = SWEEPS * step
            scale(step, 0, p0, outer, lambda k, c, t: v[p0, k, c, rows(t)])

            def sweep(i, _):
                def part(q, _):
                    for r in range(WIDE):
                        k = WIDE * q + r

                        def put(c, t, value, k=k):
                            v[i + 1, k, c, rows(t)] = value
                        update(v, i, k, i + 1 + k, step, put)
                    return 0
                lax.fori_loop(0, outer // WIDE, part, 0)
                return 0
            lax.fori_loop(SWEEPS * step, SWEEPS * (step + 1), sweep, 0)
            return 0
        lax.fori_loop(0, FINE_STEPS, fine_step, 0)

    def mirror():
        for c in range(4):
            for t in range(4):
                u[0, 1 + inner, c, rows(t)] = swap(u[0, inner, c, rows(t)])

    def around_block(low, high, put):
        def near(x, _):
            for c in range(4):
                for t in range(4):
                    put(x, c, t, jnp.where(h0, nbr[low, x, c, packed(t)], nbr[high, x, c, packed(t)]))
                    put(planes - 1 - x, c, t, swap(
                        jnp.where(h0, nbr[high, x, c, packed(t)], nbr[low, x, c, packed(t)])))
            return 0
        lax.fori_loop(0, half, near, 0)

    def put_u(p, c, t, value):
        u[0, 1 + p, c, rows(t)] = value

    def put_v(p, c, t, value):
        v[0, p, c, rows(t)] = value

    def arrived(slot):
        remote(init, nbr.at[slot], i_ss.at[0], i_rs.at[slot], (n + 1, s)).wait_recv()

    @pl.when(n <= 1)
    def _():
        for slot in (1, 2):
            @pl.when(there[slot])
            def _(slot=slot):
                arrived(slot)
                @pl.when(n == 1)
                def _():
                    passed[slot - 1].start()
        around_block(1, 2, put_u)

        def own(p, _):
            for c in range(4):
                for t in range(4):
                    u[0, 1 + W + p, c, rows(t)] = init[p, c, packed(t)]
            return 0
        lax.fori_loop(0, half, own, 0)

    @pl.when(n > 1)
    def _():
        def own(q, _):
            f = local(clin, outer // COARSE + q)
            for r in range(COARSE):
                for c in range(4):
                    for t in range(4):
                        u[0, 1 + COARSE * q + r, c, rows(t)] = f
            return 0
        lax.fori_loop(0, inner // COARSE, own, 0)

        def far(q, _):
            f = local(clin, q)
            for r in range(COARSE):
                for c in range(4):
                    for t in range(4):
                        v[0, COARSE * q + r, c, rows(t)] = f
            return 0
        lax.fori_loop(0, outer // COARSE, far, 0)

    mirror()
    for e in range(2):
        for c in range(4):
            for t in range(4):
                v[0, outer + e, c, rows(t)] = u[0, 1 + e, c, rows(t)]
    solve_inner()

    def later(box, ss, rs, d0):
        for d in range(n_count - 1, d0 - 1, -1):
            for j in range(s_count):
                if d + j > 0:
                    yield n + d < n_count, remote(
                        box.at[n, s], box.at[n, s], ss.at[d, j], rs.at[d, j], (n + d, lax.rem(s + j, s_count)))

    def share(box, ss, rs, d0):
        means = restrict(lambda p, c, t: u[0, 1 + W + p, c, rows(t)])
        for q in range(bh):
            box[n, s, q] = means[q]
        for cond, copy in later(box, ss, rs, d0):
            @pl.when(cond)
            def _(copy=copy):
                copy.start()

    def drain(box, ss, rs, d0):
        for cond, copy in later(box, ss, rs, d0):
            @pl.when(cond)
            def _(copy=copy):
                copy.wait_send()

    def collect(box, ss, rs, distances):
        for d in distances:
            @pl.when(n - d >= 1)
            def _(d=d):
                for j in range(s_count):
                    if d + j > 0:
                        b = lax.rem(s + s_count - j, s_count)
                        remote(box.at[n - d, b], box.at[n - d, b], ss.at[d, j], rs.at[d, j], (n - d, b)).wait_recv()

    def whole(box, m):
        return spread_out(lambda b, r: box[m, b, r])

    c_shape = (cq, cy, lanes)

    @pl.when(has_prev)
    def _():
        share(m1, m1_ss, m1_rs, 0)

        @pl.when(n == 1)
        def _():
            for slot in (0, 3):
                @pl.when(there[slot])
                def _(slot=slot):
                    arrived(slot)
            around_block(0, 3, put_v)
        solve_outer()

        def correct(m, e):
            delta = c_jacobi(e * c_inv, e)
            rf = whole(m1, m + 1)
            w1[m] = rf + delta
            return delta + (rf - cst[m + 1])
        collect(m1, m1_ss, m1_rs, range(n_count - 1, 0, -1))
        e = lax.fori_loop(0, n - 1, correct, jnp.zeros(c_shape, F32))
        delta = c_jacobi(e * c_inv, e)
        dl[...] = delta
        to_line(clin, delta)

        for q in range(inner // COARSE):
            at = outer // COARSE + q
            src[at] = lookup(local(llin, at), lambda r: heat[n, r])

        def start(q, _):
            f = local(clin, outer // COARSE + q)
            for r in range(COARSE):
                for c in range(4):
                    for t in range(4):
                        u[0, 1 + COARSE * q + r, c, rows(t)] = v[W, COARSE * q + r, c, rows(t)] + f
            return 0
        lax.fori_loop(0, W // COARSE, start, 0)

        def start_own(q, _):
            f = local(clin, (outer + W) // COARSE + q)
            for r in range(COARSE):
                for c in range(4):
                    for t in range(4):
                        at = 1 + W + COARSE * q + r
                        u[0, at, c, rows(t)] = u[0, at, c, rows(t)] + f
            return 0
        lax.fori_loop(0, half // COARSE, start_own, 0)
        mirror()
        solve_inner()
        share(m2, m2_ss, m2_rs, 1)

        collect(m1, m1_ss, m1_rs, [0])
        w1[n - 1] = whole(m1, n) + dl[...]
        collect(m2, m2_ss, m2_rs, range(n_count - 1, 0, -1))

        def again(m, e):
            delta = c_jacobi(e * c_inv, e)
            rf = whole(m2, m)
            return delta + (rf - w1[m])
        e = lax.fori_loop(1, n, again, jnp.zeros(c_shape, F32))
        to_line(clin, c_jacobi(e * c_inv, e))

    @pl.when(jnp.logical_not(has_prev))
    def _():
        to_line(clin, jnp.zeros(c_shape, F32))

    def finish(q, _):
        parts = []
        f = local(clin, (outer + W) // COARSE + q // 2)
        for r in range(2):
            tiles = [[u[0, 1 + W + 2 * q + r, c, rows(t)] + f for c in range(4)] for t in range(4)]
            for side in range(2):
                for t in range(4):
                    row = []
                    for e in range(zs):
                        x, y = tiles[t][2 * e], tiles[t][2 * e + 1]
                        row.append(jnp.where(h0, x, swap(y)) if side == 0 else jnp.where(h0, swap(x), y))
                    parts.append(jnp.concatenate(row, 1))
        moved = permute(jnp.concatenate(parts, 0), from_tiles)
        for r in range(2):
            for side, plane in enumerate((2 * q + r, planes - 1 - 2 * q - r)):
                for t in range(4):
                    at = (r * 8 + side * 4 + t) * cy
                    for c in range(zs):
                        raw[c, plane, pl.ds(t, cy, stride=4), :] = moved[at:at + cy, c * lanes:(c + 1) * lanes]
        return 0
    lax.fori_loop(0, half // 2, finish, 0)
    stores = [pltpu.make_async_copy(raw.at[c], out.at[0, :, :, pl.ds(c * lanes, lanes)], in_sem.at[c])
              for c in range(zs)]
    for store in stores:
        store.start()

    for cond, copy in spreads:
        @pl.when(cond)
        def _(copy=copy):
            copy.wait_send()
    for slot in (1, 2):
        @pl.when((n == 1) & there[slot])
        def _(slot=slot):
            passed[slot - 1].wait_send()

    @pl.when(has_prev)
    def _():
        drain(m1, m1_ss, m1_rs, 0)
        drain(m2, m2_ss, m2_rs, 1)

    for store in stores:
        store.wait()


def solution(mesh):
    n_count, s_count = mesh.shape["tm"], mesh.shape["space"]

    def on_device(init, labels, rates, heat):
        planes, ny, nz = init.shape
        bx, cy, cz = labels.shape
        cx = bx * s_count
        lanes = 2 * cz
        zs = nz // lanes
        half, bh, cq = planes // 2, bx // 2, cx // 2
        pad = 2 * W // COARSE
        inner, every = W + half, 2 * W + half
        dma = pltpu.SemaphoreType.DMA

        def vm(*shape):
            return pltpu.VMEM(shape, F32)

        return pl.pallas_call(
            functools.partial(kernel, n_count, s_count),
            out_shape=jax.ShapeDtypeStruct((1, planes, ny, nz), F32),
            in_specs=[pl.BlockSpec(memory_space=pl.ANY)] * 4,
            out_specs=pl.BlockSpec(memory_space=pl.ANY),
            scratch_shapes=[
                vm(zs, planes, ny, lanes), pltpu.VMEM(labels.shape, labels.dtype),
                pltpu.SMEM((1, rates.shape[0]), F32), pltpu.SMEM(heat.shape, F32),
                dma((3 + zs,)),
                vm(half, 4, 4 * cy, lanes), vm(4, half, 4, 4 * cy, lanes),
                vm(s_count, 2 * bh, cy, lanes),
                vm(n_count, s_count, bh, cy, lanes), vm(n_count, s_count, bh, cy, lanes),
                vm(n_count, cq, cy, lanes), vm(n_count, cq, cy, lanes), vm(cq, cy, lanes),
                vm(cx + 2 * pad, cy, lanes), vm(cx + 2 * pad, cy, lanes),
                vm(every, cy, lanes), vm(every // COARSE, cy, lanes), vm(every // COARSE, cy, lanes),
                vm(2, inner + 2, 4, ROWS, lanes),
                vm(W + 1, W + 2, 4, ROWS, lanes),
                vm(2, every, 4, 4 * cy, lanes),
                dma((s_count,)), dma((s_count,)),
                dma((8,)), dma((4,)),
                dma((n_count, s_count)), dma((n_count, s_count)),
                dma((n_count, s_count)), dma((n_count, s_count)),
            ],
            compiler_params=pltpu.CompilerParams(
                collective_id=0, has_side_effects=True, vmem_limit_bytes=50 * 1024 * 1024),
            name="parareal",
        )(init, labels, rates.reshape(1, -1), heat)

    return jax.shard_map(
        on_device,
        mesh=mesh,
        in_specs=(P("space", None, None), P("space", None, None), P(), P()),
        out_specs=P("tm", "space", None, None),
        check_vma=False,
    )
```

```python
import functools

import jax
import jax.numpy as jnp
from jax import lax
from jax.experimental import pallas as pl
from jax.experimental.pallas import tpu as pltpu
from jax.sharding import PartitionSpec as P

FINE_STEPS = 2
SWEEPS = 8
C_SWEEPS = 4
W = FINE_STEPS * SWEEPS
COARSE = 4
F32 = jnp.float32
BF16 = jnp.bfloat16
MESH = pl.DeviceIdType.MESH
HI = lax.Precision.HIGHEST
UNROLL = 4
WIDE = 8

ROW = (16, 0, 8, 32)
ROWS = 40


def kernel(
    n_count, s_count,
    init_hbm, labels_hbm, rates_hbm, heat_hbm,
    out,
    raw, labels, rates, heat, in_sem,
    init, nbr, ag, m1, m2, cst, w1, dl, clin, llin, wtp, inv, src, u, v, sc,
    ag_ss, ag_rs, i_ss, i_rs, m1_ss, m1_rs, m2_ss, m2_rs,
):
    n = lax.axis_index("tm")
    s = lax.axis_index("space")
    planes, ny, nz = init_hbm.shape
    bx, cy, cz = labels_hbm.shape
    cx = bx * s_count
    cq = cx // 2
    lanes = 2 * cz
    zs = nz // lanes
    regions = rates_hbm.shape[1]
    half = planes // 2
    bh = bx // 2
    pad = 2 * W // COARSE
    inner = W + half
    outer = W
    every = outer + inner
    has_prev = n > 0

    pairs = [(labels_hbm, labels), (rates_hbm, rates), (heat_hbm, heat)]
    pairs += [(init_hbm.at[:, :, pl.ds(c * lanes, lanes)], raw.at[c]) for c in range(zs)]
    fetches = [pltpu.make_async_copy(a, b, in_sem.at[i]) for i, (a, b) in enumerate(pairs)]
    for fetch in fetches:
        fetch.start()

    total = n_count * s_count
    barrier = pltpu.get_barrier_semaphore()

    def greet(k, _):
        other = lax.rem(n * s_count + s + k, total)
        pl.semaphore_signal(
            barrier, inc=1, device_id=(other // s_count, lax.rem(other, s_count)), device_id_type=MESH)
        return 0
    lax.fori_loop(1, total, greet, 0)

    def remote(a, b, ss, rs, dev):
        return pltpu.make_async_remote_copy(
            src_ref=a, dst_ref=b, send_sem=ss, recv_sem=rs, device_id=dev, device_id_type=MESH)

    lane = lax.broadcasted_iota(jnp.int32, (cy, lanes), 1)
    h0 = lane < cz
    z_first, z_last = lane % cz == 0, lane % cz == cz - 1
    zero = jnp.zeros((cy, lanes), F32)

    def swap(x):
        return pltpu.roll(x, cz, x.ndim - 1)

    def rows(t):
        return slice(ROW[t], ROW[t] + cy)

    def packed(t):
        return slice(t * cy, (t + 1) * cy)

    def clear_v(i, _):
        for k in range(outer + 2):
            for c in range(4):
                v[i, k, c, 24:32] = zero
        return 0
    lax.fori_loop(0, W + 1, clear_v, 0)

    def clear_u(k, _):
        for i in range(2):
            for c in range(4):
                u[i, k, c, 24:32] = zero
        return 0
    lax.fori_loop(0, inner + 2, clear_u, 0)
    for i in range(2):
        for c in range(4):
            for t in range(4):
                u[i, 0, c, rows(t)] = zero
    for k in range(pad):
        for at in (k, pad + cx + k):
            clin[at] = zero
            llin[at] = zero - 1.0

    zi = lax.broadcasted_iota(jnp.int32, (nz, nz), 0)
    zj = lax.broadcasted_iota(jnp.int32, (nz, nz), 1)
    to_tiles = jnp.where(zi == 4 * (zj % cz) + zj // cz, F32(1.0), F32(0.0)).astype(BF16)
    from_tiles = jnp.where(zj == 4 * (zi % cz) + zi // cz, F32(1.0), F32(0.0)).astype(BF16)

    def permute(x, one_hot):
        high = x.astype(BF16)
        rest = x - high.astype(F32)
        middle = rest.astype(BF16)
        low = (rest - middle.astype(F32)).astype(BF16)
        parts = [jnp.dot(y, one_hot, preferred_element_type=F32) for y in (high, middle, low)]
        return (parts[0] + parts[1]) + parts[2]

    for fetch in fetches:
        fetch.wait()

    def load(q, _):
        x = jnp.concatenate([
            jnp.concatenate([raw[c, plane, pl.ds(t, cy, stride=4), :] for c in range(zs)], 1)
            for r in range(2) for plane in (2 * q + r, planes - 1 - 2 * q - r) for t in range(4)], 0)
        moved = permute(x, to_tiles)
        for r in range(2):
            for t in range(4):
                for e in range(zs):
                    a = (r * 8 + t) * cy
                    b = (r * 8 + 4 + t) * cy
                    ta = moved[a:a + cy, e * lanes:(e + 1) * lanes]
                    tb = moved[b:b + cy, e * lanes:(e + 1) * lanes]
                    init[2 * q + r, 2 * e, packed(t)] = jnp.where(h0, ta, swap(tb))
                    init[2 * q + r, 2 * e + 1, packed(t)] = jnp.where(h0, swap(ta), tb)
        return 0
    lax.fori_loop(0, half // 2, load, 0)

    def restrict(tile):
        sums = []
        for q in range(bh):
            parts = [tile(COARSE * q + r, c, t) for r in range(COARSE) for c in range(4) for t in range(4)]
            while len(parts) > 1:
                parts = [a + b for a, b in zip(parts[::2], parts[1::2])]
            sums.append(parts[0] * F32(1.0 / 64.0))
        return sums

    li = lax.broadcasted_iota(jnp.int32, (cz, lanes), 0)
    lj = lax.broadcasted_iota(jnp.int32, (cz, lanes), 1)
    spread = [jnp.where(li == lj - h * cz, F32(1.0), F32(0.0)) for h in range(2)]
    means = restrict(lambda p, c, t: init[p, c, packed(t)])
    for q in range(bh):
        ag[s, q] = means[q]
        near = labels[q].astype(F32)
        far = labels[bx - 1 - q].astype(F32)
        ag[s, bh + q] = (jnp.dot(near, spread[0], precision=HI, preferred_element_type=F32)
                         + jnp.dot(far, spread[1], precision=HI, preferred_element_type=F32))

    pl.semaphore_wait(barrier, total - 1)

    gather = []
    for j in range(1, s_count):
        copy = remote(ag.at[s], ag.at[s], ag_ss.at[j], ag_rs.at[j], (n, lax.rem(s + j, s_count)))
        copy.start()
        gather.append(copy)

    aside = min(3, n_count - 1)
    has_lo, has_hi = s > 0, s < s_count - 1

    def to_even(c):
        return c & (lax.rem(s, 2) == 0)

    def to_odd(c):
        return c & (lax.rem(s, 2) == 1)
    routes = [
        (0, 1, 2, (n == 0) & (s < s_count - 2)),
        (3, 1, -2, (n == 0) & (s > 1)),
        (1, 0, 1, to_even((n == 1) & has_hi)),
        (2, 0, -1, to_odd((n == 1) & has_lo)),
        (1, 1 - aside, 1, to_odd((n == aside) & has_hi)),
        (2, 1 - aside, -1, to_even((n == aside) & has_lo)),
    ]
    spreads = [(cond, remote(init, nbr.at[slot], i_ss.at[k], i_rs.at[slot], (n + dn, s + ds)))
               for k, (slot, dn, ds, cond) in enumerate(routes)]
    for cond, copy in spreads:
        @pl.when(cond)
        def _(copy=copy):
            copy.start()
    there = [s > 1, has_lo, has_hi, s < s_count - 2]
    passed = [remote(nbr.at[slot], nbr.at[slot], i_ss.at[6 + k], i_rs.at[slot], (n - 1, s))
              for k, slot in enumerate((1, 2))]

    for slot in range(4):
        @pl.when((n <= 1) & jnp.logical_not(there[slot]))
        def _(slot=slot):
            def wipe(p, _):
                for c in range(4):
                    for t in range(4):
                        nbr[slot, p, c, packed(t)] = zero
                return 0
            lax.fori_loop(0, half, wipe, 0)

    for copy in gather:
        copy.wait()

    def spread_out(block):
        parts = []
        for q in range(cq):
            b, r = q // bx, q % bx
            if r < bh:
                parts.append(jnp.where(h0, block(b, r), block(s_count - 1 - b, r)))
            else:
                at = bx - 1 - r
                parts.append(swap(jnp.where(h0, block(s_count - 1 - b, at), block(b, at))))
        return jnp.stack(parts, 0)

    def to_line(ref, g):
        for q in range(cq):
            x, y = g[q], swap(g[q])
            ref[pad + q] = jnp.where(h0, x, y)
            ref[pad + cx - 1 - q] = jnp.where(h0, y, x)

    def local(ref, q):
        return jnp.where(h0, ref[bx * s + q], ref[bx * s + bx + 2 * pad - 1 - q])

    def lookup(lab, row):
        value = jnp.zeros(lab.shape, F32)
        for r in range(regions):
            value = value + jnp.where(lab == F32(r), row(r), F32(0.0))
        return value

    crow = lax.broadcasted_iota(jnp.int32, (cq, cy, lanes), 1)
    ccol = lax.broadcasted_iota(jnp.int32, (cq, cy, lanes), 2)
    c_first, c_last = crow == 0, crow == cy - 1
    cz_first, cz_last = ccol % cz == 0, ccol % cz == cz - 1
    czero = jnp.zeros((1, cy, lanes), F32)

    def c_neighbours(x):
        value = (jnp.concatenate([czero, x[:-1]], 0)
                 + jnp.concatenate([x[1:], swap(x[-1:])], 0))
        value = value + (jnp.where(c_first, F32(0.0), pltpu.roll(x, 1, 1))
                         + jnp.where(c_last, F32(0.0), pltpu.roll(x, cy - 1, 1)))
        return value + (jnp.where(cz_first, F32(0.0), pltpu.roll(x, 1, 2))
                        + jnp.where(cz_last, F32(0.0), pltpu.roll(x, lanes - 1, 2)))

    lab_all = spread_out(lambda b, r: ag[b, bh + r])
    c_rate = FINE_STEPS * lookup(lab_all, lambda r: rates[0, r]) / 16.0
    c_inv = 1.0 / (1.0 + 6.0 * c_rate)
    c_weight = c_rate * c_inv

    def c_jacobi(scaled, x):
        for _ in range(C_SWEEPS):
            x = scaled + c_weight * c_neighbours(x)
        return x

    cst[0] = spread_out(lambda b, r: ag[b, r])

    def advance(m, c):
        source = FINE_STEPS * lookup(lab_all, lambda r: heat[m, r])
        c = c_jacobi((c + source) * c_inv, c)
        cst[m + 1] = c
        return c

    to_line(llin, lab_all)

    @pl.when(n > 1)
    def _():
        to_line(clin, lax.fori_loop(0, n - 1, advance, cst[0]))
    slice_of_a = n - jnp.where(has_prev, 1, 0).astype(jnp.int32)

    for q in range(every // COARSE):
        lab = local(llin, q)
        rate = lookup(lab, lambda r: rates[0, r])
        iv = 1.0 / (1.0 + 6.0 * rate)
        inv[q] = iv
        src[q] = lookup(lab, lambda r: heat[slice_of_a, r])
        for r in range(COARSE):
            wtp[COARSE * q + r] = rate * iv

    def update(ref, level, k, p, step, put):
        def get(at, t, c):
            return ref[level, at, c, rows(t)]
        below, here, above = k, k + 1, k + 2
        g = [[ref[level, here, c, ROW[3] - 1:ROW[3] - 1 + cy] for c in range(4)]]
        g += [[get(here, t, c) for c in range(4)] for t in range(4)]
        g += [[ref[level, here, c, ROW[0] + 1:ROW[0] + 1 + cy] for c in range(4)]]
        for t in range(4):
            g[t + 1].append(jnp.where(z_last, F32(0.0), pltpu.roll(g[t + 1][0], lanes - 1, 1)))
        d = [[g[a + 1][b + 1] + g[a + 2][b] if a >= 0 or b < 3 else None for b in range(4)] for a in range(-1, 4)]
        left = [g[a + 1][0] + jnp.where(z_first, F32(0.0), pltpu.roll(g[a + 2][3], 1, 1)) for a in range(-1, 3)]
        we = wtp[p]
        for t in range(4):
            for c in range(4):
                around = d[t + 1][c] + (left[t] if c == 0 else d[t][c - 1])
                around = around + (get(below, t, c) + get(above, t, c))
                put(c, t, sc[step, p, c, packed(t)] + we * around)

    def scale(step, first, p0, count, plane):
        def quad(q, _):
            iv, so = inv[p0 // COARSE + q], src[p0 // COARSE + q]
            for r in range(COARSE):
                for c in range(4):
                    for t in range(4):
                        sc[step, p0 + COARSE * q + r, c, packed(t)] = (plane(COARSE * q + r, c, t) + so) * iv
            return 0
        lax.fori_loop(first, count // COARSE, quad, 0)

    def solve_inner():
        def fine_step(step, _):
            scale(step, SWEEPS // COARSE * step, outer, inner, lambda p, c, t: u[0, 1 + p, c, rows(t)])

            def sweep(i, now):
                then = 1 - now

                def block(p0, count, edge):
                    for r in range(count):
                        p = p0 + r

                        def put(c, t, value, p=p, r=r):
                            u[then, 1 + p, c, rows(t)] = value
                            if edge and r == count - 1:
                                u[then, 2 + p, c, rows(t)] = swap(value)
                        update(u, now, p, outer + p, step, put)
                    return 0
                first = (1 + i) // UNROLL
                lax.fori_loop(first, first + lax.rem(first, 2), lambda q, _: block(UNROLL * q, UNROLL, False), 0)
                lax.fori_loop((first + 1) // 2, inner // WIDE - 1, lambda q, _: block(WIDE * q, WIDE, False), 0)
                block(inner - WIDE, WIDE, True)
                for e in range(2):
                    for c in range(4):
                        for t in range(4):
                            v[i + 1, outer + e, c, rows(t)] = u[then, 2 + i + e, c, rows(t)]

            def two(j, _):
                sweep(SWEEPS * step + 2 * j, 0)
                sweep(SWEEPS * step + 2 * j + 1, 1)
                return 0
            lax.fori_loop(0, SWEEPS // 2, two, 0)
            return 0
        lax.fori_loop(0, FINE_STEPS, fine_step, 0)

    def solve_outer():
        def fine_step(step, _):
            p0 = SWEEPS * step
            scale(step, 0, p0, outer, lambda k, c, t: v[p0, k, c, rows(t)])

            def sweep(i, _):
                def part(q, _):
                    for r in range(WIDE):
                        k = WIDE * q + r

                        def put(c, t, value, k=k):
                            v[i + 1, k, c, rows(t)] = value
                        update(v, i, k, i + 1 + k, step, put)
                    return 0
                lax.fori_loop(0, outer // WIDE, part, 0)
                return 0
            lax.fori_loop(SWEEPS * step, SWEEPS * (step + 1), sweep, 0)
            return 0
        lax.fori_loop(0, FINE_STEPS, fine_step, 0)

    def mirror():
        for c in range(4):
            for t in range(4):
                u[0, 1 + inner, c, rows(t)] = swap(u[0, inner, c, rows(t)])

    def around_block(low, high, put):
        def near(x, _):
            for c in range(4):
                for t in range(4):
                    put(x, c, t, jnp.where(h0, nbr[low, x, c, packed(t)], nbr[high, x, c, packed(t)]))
                    put(planes - 1 - x, c, t, swap(
                        jnp.where(h0, nbr[high, x, c, packed(t)], nbr[low, x, c, packed(t)])))
            return 0
        lax.fori_loop(0, half, near, 0)

    def put_u(p, c, t, value):
        u[0, 1 + p, c, rows(t)] = value

    def put_v(p, c, t, value):
        v[0, p, c, rows(t)] = value

    def arrived(slot):
        remote(init, nbr.at[slot], i_ss.at[0], i_rs.at[slot], (n + 1, s)).wait_recv()

    @pl.when(n <= 1)
    def _():
        for slot in (1, 2):
            @pl.when(there[slot])
            def _(slot=slot):
                arrived(slot)
                @pl.when(n == 1)
                def _():
                    passed[slot - 1].start()
        around_block(1, 2, put_u)

        def own(p, _):
            for c in range(4):
                for t in range(4):
                    u[0, 1 + W + p, c, rows(t)] = init[p, c, packed(t)]
            return 0
        lax.fori_loop(0, half, own, 0)

    @pl.when(n > 1)
    def _():
        def own(q, _):
            f = local(clin, outer // COARSE + q)
            for r in range(COARSE):
                for c in range(4):
                    for t in range(4):
                        u[0, 1 + COARSE * q + r, c, rows(t)] = f
            return 0
        lax.fori_loop(0, inner // COARSE, own, 0)

        def far(q, _):
            f = local(clin, q)
            for r in range(COARSE):
                for c in range(4):
                    for t in range(4):
                        v[0, COARSE * q + r, c, rows(t)] = f
            return 0
        lax.fori_loop(0, outer // COARSE, far, 0)

    mirror()
    for e in range(2):
        for c in range(4):
            for t in range(4):
                v[0, outer + e, c, rows(t)] = u[0, 1 + e, c, rows(t)]
    solve_inner()

    def later(box, ss, rs, d0):
        for d in range(n_count - 1, d0 - 1, -1):
            for j in range(s_count):
                if d + j > 0:
                    yield n + d < n_count, remote(
                        box.at[n, s], box.at[n, s], ss.at[d, j], rs.at[d, j], (n + d, lax.rem(s + j, s_count)))

    def share(box, ss, rs, d0):
        means = restrict(lambda p, c, t: u[0, 1 + W + p, c, rows(t)])
        for q in range(bh):
            box[n, s, q] = means[q]
        for cond, copy in later(box, ss, rs, d0):
            @pl.when(cond)
            def _(copy=copy):
                copy.start()

    def drain(box, ss, rs, d0):
        for cond, copy in later(box, ss, rs, d0):
            @pl.when(cond)
            def _(copy=copy):
                copy.wait_send()

    def collect(box, ss, rs, distances):
        for d in distances:
            @pl.when(n - d >= 1)
            def _(d=d):
                for j in range(s_count):
                    if d + j > 0:
                        b = lax.rem(s + s_count - j, s_count)
                        remote(box.at[n - d, b], box.at[n - d, b], ss.at[d, j], rs.at[d, j], (n - d, b)).wait_recv()

    def whole(box, m):
        return spread_out(lambda b, r: box[m, b, r])

    c_shape = (cq, cy, lanes)

    @pl.when(has_prev)
    def _():
        share(m1, m1_ss, m1_rs, 0)

        @pl.when(n == 1)
        def _():
            for slot in (0, 3):
                @pl.when(there[slot])
                def _(slot=slot):
                    arrived(slot)
            around_block(0, 3, put_v)
        solve_outer()

        def correct(m, e):
            delta = c_jacobi(e * c_inv, e)
            rf = whole(m1, m + 1)
            w1[m] = rf + delta
            return delta + (rf - cst[m + 1])
        collect(m1, m1_ss, m1_rs, range(n_count - 1, 0, -1))
        e = lax.fori_loop(0, n - 1, correct, jnp.zeros(c_shape, F32))
        delta = c_jacobi(e * c_inv, e)
        dl[...] = delta
        to_line(clin, delta)

        for q in range(inner // COARSE):
            at = outer // COARSE + q
            src[at] = lookup(local(llin, at), lambda r: heat[n, r])

        def start(q, _):
            f = local(clin, outer // COARSE + q)
            for r in range(COARSE):
                for c in range(4):
                    for t in range(4):
                        u[0, 1 + COARSE * q + r, c, rows(t)] = v[W, COARSE * q + r, c, rows(t)] + f
            return 0
        lax.fori_loop(0, W // COARSE, start, 0)

        def start_own(q, _):
            f = local(clin, (outer + W) // COARSE + q)
            for r in range(COARSE):
                for c in range(4):
                    for t in range(4):
                        at = 1 + W + COARSE * q + r
                        u[0, at, c, rows(t)] = u[0, at, c, rows(t)] + f
            return 0
        lax.fori_loop(0, half // COARSE, start_own, 0)
        mirror()
        solve_inner()
        share(m2, m2_ss, m2_rs, 1)

        drain(m1, m1_ss, m1_rs, 0)
        collect(m1, m1_ss, m1_rs, [0])
        w1[n - 1] = whole(m1, n) + dl[...]
        collect(m2, m2_ss, m2_rs, range(n_count - 1, 0, -1))
        drain(m2, m2_ss, m2_rs, 1)

        def again(m, e):
            delta = c_jacobi(e * c_inv, e)
            rf = whole(m2, m)
            return delta + (rf - w1[m])
        e = lax.fori_loop(1, n, again, jnp.zeros(c_shape, F32))
        to_line(clin, c_jacobi(e * c_inv, e))

    @pl.when(jnp.logical_not(has_prev))
    def _():
        to_line(clin, jnp.zeros(c_shape, F32))

    def finish(q, _):
        parts = []
        f = local(clin, (outer + W) // COARSE + q // 2)
        for r in range(2):
            tiles = [[u[0, 1 + W + 2 * q + r, c, rows(t)] + f for c in range(4)] for t in range(4)]
            for side in range(2):
                for t in range(4):
                    row = []
                    for e in range(zs):
                        x, y = tiles[t][2 * e], tiles[t][2 * e + 1]
                        row.append(jnp.where(h0, x, swap(y)) if side == 0 else jnp.where(h0, swap(x), y))
                    parts.append(jnp.concatenate(row, 1))
        moved = permute(jnp.concatenate(parts, 0), from_tiles)
        for r in range(2):
            for side, plane in enumerate((2 * q + r, planes - 1 - 2 * q - r)):
                for t in range(4):
                    at = (r * 8 + side * 4 + t) * cy
                    for c in range(zs):
                        raw[c, plane, pl.ds(t, cy, stride=4), :] = moved[at:at + cy, c * lanes:(c + 1) * lanes]
        return 0
    lax.fori_loop(0, half // 2, finish, 0)
    stores = [pltpu.make_async_copy(raw.at[c], out.at[0, :, :, pl.ds(c * lanes, lanes)], in_sem.at[c])
              for c in range(zs)]
    for store in stores:
        store.start()

    for cond, copy in spreads:
        @pl.when(cond)
        def _(copy=copy):
            copy.wait_send()
    for slot in (1, 2):
        @pl.when((n == 1) & there[slot])
        def _(slot=slot):
            passed[slot - 1].wait_send()

    for store in stores:
        store.wait()


def solution(mesh):
    n_count, s_count = mesh.shape["tm"], mesh.shape["space"]

    def on_device(init, labels, rates, heat):
        planes, ny, nz = init.shape
        bx, cy, cz = labels.shape
        cx = bx * s_count
        lanes = 2 * cz
        zs = nz // lanes
        half, bh, cq = planes // 2, bx // 2, cx // 2
        pad = 2 * W // COARSE
        inner, every = W + half, 2 * W + half
        dma = pltpu.SemaphoreType.DMA

        def vm(*shape):
            return pltpu.VMEM(shape, F32)

        return pl.pallas_call(
            functools.partial(kernel, n_count, s_count),
            out_shape=jax.ShapeDtypeStruct((1, planes, ny, nz), F32),
            in_specs=[pl.BlockSpec(memory_space=pl.ANY)] * 4,
            out_specs=pl.BlockSpec(memory_space=pl.ANY),
            scratch_shapes=[
                vm(zs, planes, ny, lanes), pltpu.VMEM(labels.shape, labels.dtype),
                pltpu.SMEM((1, rates.shape[0]), F32), pltpu.SMEM(heat.shape, F32),
                dma((3 + zs,)),
                vm(half, 4, 4 * cy, lanes), vm(4, half, 4, 4 * cy, lanes),
                vm(s_count, 2 * bh, cy, lanes),
                vm(n_count, s_count, bh, cy, lanes), vm(n_count, s_count, bh, cy, lanes),
                vm(n_count, cq, cy, lanes), vm(n_count, cq, cy, lanes), vm(cq, cy, lanes),
                vm(cx + 2 * pad, cy, lanes), vm(cx + 2 * pad, cy, lanes),
                vm(every, cy, lanes), vm(every // COARSE, cy, lanes), vm(every // COARSE, cy, lanes),
                vm(2, inner + 2, 4, ROWS, lanes),
                vm(W + 1, W + 2, 4, ROWS, lanes),
                vm(2, every, 4, 4 * cy, lanes),
                dma((s_count,)), dma((s_count,)),
                dma((8,)), dma((4,)),
                dma((n_count, s_count)), dma((n_count, s_count)),
                dma((n_count, s_count)), dma((n_count, s_count)),
            ],
            compiler_params=pltpu.CompilerParams(
                collective_id=0, has_side_effects=True, vmem_limit_bytes=67_043_328),
            name="parareal",
        )(init, labels, rates.reshape(1, -1), heat)

    return jax.shard_map(
        on_device,
        mesh=mesh,
        in_specs=(P("space", None, None), P("space", None, None), P(), P()),
        out_specs=P("tm", "space", None, None),
        check_vma=False,
    )
```

```python
import functools

import jax
import jax.numpy as jnp
from jax import lax
from jax.experimental import pallas as pl
from jax.experimental.pallas import tpu as pltpu
from jax.sharding import PartitionSpec as P

FINE_STEPS = 2
SWEEPS = 8
C_SWEEPS = 4
W = FINE_STEPS * SWEEPS
COARSE = 4
F32 = jnp.float32
BF16 = jnp.bfloat16
MESH = pl.DeviceIdType.MESH
HI = lax.Precision.HIGHEST
UNROLL = 4
WIDE = 8

ROW = (16, 0, 8, 32)
ROWS = 40


def kernel(
    n_count, s_count,
    init_hbm, labels_hbm, rates_hbm, heat_hbm,
    out,
    raw, labels, rates, heat, in_sem,
    init, nbr, ag, m1, m2, cst, w1, dl, clin, llin, wtp, inv, src, u, v, sc,
    ag_ss, ag_rs, i_ss, i_rs, m1_ss, m1_rs, m2_ss, m2_rs,
):
    n = lax.axis_index("tm")
    s = lax.axis_index("space")
    planes, ny, nz = init_hbm.shape
    bx, cy, cz = labels_hbm.shape
    cx = bx * s_count
    cq = cx // 2
    lanes = 2 * cz
    zs = nz // lanes
    regions = rates_hbm.shape[1]
    half = planes // 2
    bh = bx // 2
    pad = 2 * W // COARSE
    inner = W + half
    outer = W
    every = outer + inner
    has_prev = n > 0

    pairs = [(labels_hbm, labels), (rates_hbm, rates), (heat_hbm, heat)]
    pairs += [(init_hbm.at[:, :, pl.ds(c * lanes, lanes)], raw.at[c]) for c in range(zs)]
    fetches = [pltpu.make_async_copy(a, b, in_sem.at[i]) for i, (a, b) in enumerate(pairs)]
    for fetch in fetches:
        fetch.start()

    total = n_count * s_count
    barrier = pltpu.get_barrier_semaphore()

    def greet(k, _):
        other = lax.rem(n * s_count + s + k, total)
        pl.semaphore_signal(
            barrier, inc=1, device_id=(other // s_count, lax.rem(other, s_count)), device_id_type=MESH)
        return 0
    lax.fori_loop(1, total, greet, 0)

    def remote(a, b, ss, rs, dev):
        return pltpu.make_async_remote_copy(
            src_ref=a, dst_ref=b, send_sem=ss, recv_sem=rs, device_id=dev, device_id_type=MESH)

    lane = lax.broadcasted_iota(jnp.int32, (cy, lanes), 1)
    h0 = lane < cz
    z_first, z_last = lane % cz == 0, lane % cz == cz - 1
    zero = jnp.zeros((cy, lanes), F32)

    def swap(x):
        return pltpu.roll(x, cz, x.ndim - 1)

    def rows(t):
        return slice(ROW[t], ROW[t] + cy)

    def packed(t):
        return slice(t * cy, (t + 1) * cy)

    def clear_v(i, _):
        for k in range(outer + 2):
            for c in range(4):
                v[i, k, c, 24:32] = zero
        return 0
    lax.fori_loop(0, W + 1, clear_v, 0)

    def clear_u(k, _):
        for i in range(2):
            for c in range(4):
                u[i, k, c, 24:32] = zero
        return 0
    lax.fori_loop(0, inner + 2, clear_u, 0)
    for i in range(2):
        for c in range(4):
            for t in range(4):
                u[i, 0, c, rows(t)] = zero
    for k in range(pad):
        for at in (k, pad + cx + k):
            clin[at] = zero
            llin[at] = zero - 1.0

    zi = lax.broadcasted_iota(jnp.int32, (nz, nz), 0)
    zj = lax.broadcasted_iota(jnp.int32, (nz, nz), 1)
    to_tiles = jnp.where(zi == 4 * (zj % cz) + zj // cz, F32(1.0), F32(0.0)).astype(BF16)
    from_tiles = jnp.where(zj == 4 * (zi % cz) + zi // cz, F32(1.0), F32(0.0)).astype(BF16)

    def permute(x, one_hot):
        high = x.astype(BF16)
        rest = x - high.astype(F32)
        middle = rest.astype(BF16)
        low = (rest - middle.astype(F32)).astype(BF16)
        parts = [jnp.dot(y, one_hot, preferred_element_type=F32) for y in (high, middle, low)]
        return (parts[0] + parts[1]) + parts[2]

    for fetch in fetches:
        fetch.wait()

    def load(q, _):
        x = jnp.concatenate([
            jnp.concatenate([raw[c, plane, pl.ds(t, cy, stride=4), :] for c in range(zs)], 1)
            for r in range(2) for plane in (2 * q + r, planes - 1 - 2 * q - r) for t in range(4)], 0)
        moved = permute(x, to_tiles)
        for r in range(2):
            for t in range(4):
                for e in range(zs):
                    a = (r * 8 + t) * cy
                    b = (r * 8 + 4 + t) * cy
                    ta = moved[a:a + cy, e * lanes:(e + 1) * lanes]
                    tb = moved[b:b + cy, e * lanes:(e + 1) * lanes]
                    init[2 * q + r, 2 * e, packed(t)] = jnp.where(h0, ta, swap(tb))
                    init[2 * q + r, 2 * e + 1, packed(t)] = jnp.where(h0, swap(ta), tb)
        return 0
    lax.fori_loop(0, half // 2, load, 0)

    def restrict(tile):
        sums = []
        for q in range(bh):
            parts = [tile(COARSE * q + r, c, t) for r in range(COARSE) for c in range(4) for t in range(4)]
            while len(parts) > 1:
                parts = [a + b for a, b in zip(parts[::2], parts[1::2])]
            sums.append(parts[0] * F32(1.0 / 64.0))
        return sums

    li = lax.broadcasted_iota(jnp.int32, (cz, lanes), 0)
    lj = lax.broadcasted_iota(jnp.int32, (cz, lanes), 1)
    spread = [jnp.where(li == lj - h * cz, F32(1.0), F32(0.0)) for h in range(2)]
    means = restrict(lambda p, c, t: init[p, c, packed(t)])
    for q in range(bh):
        ag[s, q] = means[q]
        near = labels[q].astype(F32)
        far = labels[bx - 1 - q].astype(F32)
        ag[s, bh + q] = (jnp.dot(near, spread[0], precision=HI, preferred_element_type=F32)
                         + jnp.dot(far, spread[1], precision=HI, preferred_element_type=F32))

    pl.semaphore_wait(barrier, total - 1)

    gather = []
    for j in range(1, s_count):
        copy = remote(ag.at[s], ag.at[s], ag_ss.at[j], ag_rs.at[j], (n, lax.rem(s + j, s_count)))
        copy.start()
        gather.append(copy)

    aside = min(3, n_count - 1)
    has_lo, has_hi = s > 0, s < s_count - 1

    def to_even(c):
        return c & (lax.rem(s, 2) == 0)

    def to_odd(c):
        return c & (lax.rem(s, 2) == 1)
    routes = [
        (0, 1, 2, (n == 0) & (s < s_count - 2)),
        (3, 1, -2, (n == 0) & (s > 1)),
        (1, 0, 1, to_even((n == 1) & has_hi)),
        (2, 0, -1, to_odd((n == 1) & has_lo)),
        (1, 1 - aside, 1, to_odd((n == aside) & has_hi)),
        (2, 1 - aside, -1, to_even((n == aside) & has_lo)),
    ]
    spreads = [(cond, remote(init, nbr.at[slot], i_ss.at[k], i_rs.at[slot], (n + dn, s + ds)))
               for k, (slot, dn, ds, cond) in enumerate(routes)]
    for cond, copy in spreads:
        @pl.when(cond)
        def _(copy=copy):
            copy.start()
    there = [s > 1, has_lo, has_hi, s < s_count - 2]
    passed = [remote(nbr.at[slot], nbr.at[slot], i_ss.at[6 + k], i_rs.at[slot], (n - 1, s))
              for k, slot in enumerate((1, 2))]

    for slot in range(4):
        @pl.when((n <= 1) & jnp.logical_not(there[slot]))
        def _(slot=slot):
            def wipe(p, _):
                for c in range(4):
                    for t in range(4):
                        nbr[slot, p, c, packed(t)] = zero
                return 0
            lax.fori_loop(0, half, wipe, 0)

    for copy in gather:
        copy.wait()

    def spread_out(block):
        parts = []
        for q in range(cq):
            b, r = q // bx, q % bx
            if r < bh:
                parts.append(jnp.where(h0, block(b, r), block(s_count - 1 - b, r)))
            else:
                at = bx - 1 - r
                parts.append(swap(jnp.where(h0, block(s_count - 1 - b, at), block(b, at))))
        return jnp.stack(parts, 0)

    def to_line(ref, g):
        for q in range(cq):
            x, y = g[q], swap(g[q])
            ref[pad + q] = jnp.where(h0, x, y)
            ref[pad + cx - 1 - q] = jnp.where(h0, y, x)

    def local(ref, q):
        return jnp.where(h0, ref[bx * s + q], ref[bx * s + bx + 2 * pad - 1 - q])

    def lookup(lab, row):
        value = jnp.zeros(lab.shape, F32)
        for r in range(regions):
            value = value + jnp.where(lab == F32(r), row(r), F32(0.0))
        return value

    crow = lax.broadcasted_iota(jnp.int32, (cq, cy, lanes), 1)
    ccol = lax.broadcasted_iota(jnp.int32, (cq, cy, lanes), 2)
    c_first, c_last = crow == 0, crow == cy - 1
    cz_first, cz_last = ccol % cz == 0, ccol % cz == cz - 1
    czero = jnp.zeros((1, cy, lanes), F32)

    def c_neighbours(x):
        value = (jnp.concatenate([czero, x[:-1]], 0)
                 + jnp.concatenate([x[1:], swap(x[-1:])], 0))
        value = value + (jnp.where(c_first, F32(0.0), pltpu.roll(x, 1, 1))
                         + jnp.where(c_last, F32(0.0), pltpu.roll(x, cy - 1, 1)))
        return value + (jnp.where(cz_first, F32(0.0), pltpu.roll(x, 1, 2))
                        + jnp.where(cz_last, F32(0.0), pltpu.roll(x, lanes - 1, 2)))

    lab_all = spread_out(lambda b, r: ag[b, bh + r])
    c_rate = FINE_STEPS * lookup(lab_all, lambda r: rates[0, r]) / 16.0
    c_inv = 1.0 / (1.0 + 6.0 * c_rate)
    c_weight = c_rate * c_inv

    def c_jacobi(scaled, x):
        for _ in range(C_SWEEPS):
            x = scaled + c_weight * c_neighbours(x)
        return x

    cst[0] = spread_out(lambda b, r: ag[b, r])

    def advance(m, c):
        source = FINE_STEPS * lookup(lab_all, lambda r: heat[m, r])
        c = c_jacobi((c + source) * c_inv, c)
        cst[m + 1] = c
        return c

    to_line(llin, lab_all)

    @pl.when(n > 1)
    def _():
        to_line(clin, lax.fori_loop(0, n - 1, advance, cst[0]))
    slice_of_a = n - jnp.where(has_prev, 1, 0).astype(jnp.int32)

    for q in range(every // COARSE):
        lab = local(llin, q)
        rate = lookup(lab, lambda r: rates[0, r])
        iv = 1.0 / (1.0 + 6.0 * rate)
        inv[q] = iv
        src[q] = lookup(lab, lambda r: heat[slice_of_a, r])
        for r in range(COARSE):
            wtp[COARSE * q + r] = rate * iv

    def update(ref, level, k, p, step, put):
        def get(at, t, c):
            return ref[level, at, c, rows(t)]
        below, here, above = k, k + 1, k + 2
        g = [[ref[level, here, c, ROW[3] - 1:ROW[3] - 1 + cy] for c in range(4)]]
        g += [[get(here, t, c) for c in range(4)] for t in range(4)]
        g += [[ref[level, here, c, ROW[0] + 1:ROW[0] + 1 + cy] for c in range(4)]]
        for t in range(4):
            g[t + 1].append(jnp.where(z_last, F32(0.0), pltpu.roll(g[t + 1][0], lanes - 1, 1)))
        d = [[g[a + 1][b + 1] + g[a + 2][b] if a >= 0 or b < 3 else None for b in range(4)] for a in range(-1, 4)]
        left = [g[a + 1][0] + jnp.where(z_first, F32(0.0), pltpu.roll(g[a + 2][3], 1, 1)) for a in range(-1, 3)]
        we = wtp[p]
        for t in range(4):
            for c in range(4):
                around = d[t + 1][c] + (left[t] if c == 0 else d[t][c - 1])
                around = around + (get(below, t, c) + get(above, t, c))
                put(c, t, sc[step, p, c, packed(t)] + we * around)

    def scale(step, first, p0, count, plane):
        def quad(q, _):
            iv, so = inv[p0 // COARSE + q], src[p0 // COARSE + q]
            for r in range(COARSE):
                for c in range(4):
                    for t in range(4):
                        sc[step, p0 + COARSE * q + r, c, packed(t)] = (plane(COARSE * q + r, c, t) + so) * iv
            return 0
        lax.fori_loop(first, count // COARSE, quad, 0)

    def solve_inner():
        def fine_step(step, _):
            scale(step, SWEEPS // COARSE * step, outer, inner, lambda p, c, t: u[0, 1 + p, c, rows(t)])

            def sweep(i, now):
                then = 1 - now

                def block(p0, count, edge):
                    for r in range(count):
                        p = p0 + r

                        def put(c, t, value, p=p, r=r):
                            u[then, 1 + p, c, rows(t)] = value
                            if edge and r == count - 1:
                                u[then, 2 + p, c, rows(t)] = swap(value)
                        update(u, now, p, outer + p, step, put)
                    return 0
                first = (1 + i) // UNROLL
                lax.fori_loop(first, first + lax.rem(first, 2), lambda q, _: block(UNROLL * q, UNROLL, False), 0)
                lax.fori_loop((first + 1) // 2, inner // WIDE - 1, lambda q, _: block(WIDE * q, WIDE, False), 0)
                block(inner - WIDE, WIDE, True)
                for e in range(2):
                    for c in range(4):
                        for t in range(4):
                            v[i + 1, outer + e, c, rows(t)] = u[then, 2 + i + e, c, rows(t)]

            def two(j, _):
                sweep(SWEEPS * step + 2 * j, 0)
                sweep(SWEEPS * step + 2 * j + 1, 1)
                return 0
            lax.fori_loop(0, SWEEPS // 2, two, 0)
            return 0
        lax.fori_loop(0, FINE_STEPS, fine_step, 0)

    def solve_outer():
        def fine_step(step, _):
            p0 = SWEEPS * step
            scale(step, 0, p0, outer, lambda k, c, t: v[p0, k, c, rows(t)])

            def sweep(i, _):
                def part(q, _):
                    for r in range(WIDE):
                        k = WIDE * q + r

                        def put(c, t, value, k=k):
                            v[i + 1, k, c, rows(t)] = value
                        update(v, i, k, i + 1 + k, step, put)
                    return 0
                lax.fori_loop(0, outer // WIDE, part, 0)
                return 0
            lax.fori_loop(SWEEPS * step, SWEEPS * (step + 1), sweep, 0)
            return 0
        lax.fori_loop(0, FINE_STEPS, fine_step, 0)

    def mirror():
        for c in range(4):
            for t in range(4):
                u[0, 1 + inner, c, rows(t)] = swap(u[0, inner, c, rows(t)])

    def around_block(low, high, put):
        def near(x, _):
            for c in range(4):
                for t in range(4):
                    put(x, c, t, jnp.where(h0, nbr[low, x, c, packed(t)], nbr[high, x, c, packed(t)]))
                    put(planes - 1 - x, c, t, swap(
                        jnp.where(h0, nbr[high, x, c, packed(t)], nbr[low, x, c, packed(t)])))
            return 0
        lax.fori_loop(0, half, near, 0)

    def put_u(p, c, t, value):
        u[0, 1 + p, c, rows(t)] = value

    def put_v(p, c, t, value):
        v[0, p, c, rows(t)] = value

    def arrived(slot):
        remote(init, nbr.at[slot], i_ss.at[0], i_rs.at[slot], (n + 1, s)).wait_recv()

    @pl.when(n <= 1)
    def _():
        for slot in (1, 2):
            @pl.when(there[slot])
            def _(slot=slot):
                arrived(slot)
                @pl.when(n == 1)
                def _():
                    passed[slot - 1].start()
        around_block(1, 2, put_u)

        def own(p, _):
            for c in range(4):
                for t in range(4):
                    u[0, 1 + W + p, c, rows(t)] = init[p, c, packed(t)]
            return 0
        lax.fori_loop(0, half, own, 0)

    @pl.when(n > 1)
    def _():
        def own(q, _):
            f = local(clin, outer // COARSE + q)
            for r in range(COARSE):
                for c in range(4):
                    for t in range(4):
                        u[0, 1 + COARSE * q + r, c, rows(t)] = f
            return 0
        lax.fori_loop(0, inner // COARSE, own, 0)

        def far(q, _):
            f = local(clin, q)
            for r in range(COARSE):
                for c in range(4):
                    for t in range(4):
                        v[0, COARSE * q + r, c, rows(t)] = f
            return 0
        lax.fori_loop(0, outer // COARSE, far, 0)

    mirror()
    for e in range(2):
        for c in range(4):
            for t in range(4):
                v[0, outer + e, c, rows(t)] = u[0, 1 + e, c, rows(t)]
    solve_inner()

    def later(box, ss, rs, d0):
        for d in range(n_count - 1, d0 - 1, -1):
            for j in range(s_count):
                if d + j > 0:
                    yield n + d < n_count, remote(
                        box.at[n, s], box.at[n, s], ss.at[d, j], rs.at[d, j], (n + d, lax.rem(s + j, s_count)))

    def share(box, ss, rs, d0):
        means = restrict(lambda p, c, t: u[0, 1 + W + p, c, rows(t)])
        for q in range(bh):
            box[n, s, q] = means[q]
        for cond, copy in later(box, ss, rs, d0):
            @pl.when(cond)
            def _(copy=copy):
                copy.start()

    def drain(box, ss, rs, d0):
        for cond, copy in later(box, ss, rs, d0):
            @pl.when(cond)
            def _(copy=copy):
                copy.wait_send()

    def collect(box, ss, rs, distances):
        for d in distances:
            @pl.when(n - d >= 1)
            def _(d=d):
                for j in range(s_count):
                    if d + j > 0:
                        b = lax.rem(s + s_count - j, s_count)
                        remote(box.at[n - d, b], box.at[n - d, b], ss.at[d, j], rs.at[d, j], (n - d, b)).wait_recv()

    def whole(box, m):
        return spread_out(lambda b, r: box[m, b, r])

    c_shape = (cq, cy, lanes)

    @pl.when(has_prev)
    def _():
        share(m1, m1_ss, m1_rs, 0)

        @pl.when(n == 1)
        def _():
            for slot in (0, 3):
                @pl.when(there[slot])
                def _(slot=slot):
                    arrived(slot)
            around_block(0, 3, put_v)
        solve_outer()

        def correct(m, e):
            delta = c_jacobi(e * c_inv, e)
            rf = whole(m1, m + 1)
            w1[m] = rf + delta
            return delta + (rf - cst[m + 1])
        collect(m1, m1_ss, m1_rs, range(n_count - 1, 0, -1))
        e = lax.fori_loop(0, n - 1, correct, jnp.zeros(c_shape, F32))
        delta = c_jacobi(e * c_inv, e)
        dl[...] = delta
        to_line(clin, delta)

        for q in range(inner // COARSE):
            at = outer // COARSE + q
            src[at] = lookup(local(llin, at), lambda r: heat[n, r])

        def start(q, _):
            f = local(clin, outer // COARSE + q)
            for r in range(COARSE):
                for c in range(4):
                    for t in range(4):
                        u[0, 1 + COARSE * q + r, c, rows(t)] = v[W, COARSE * q + r, c, rows(t)] + f
            return 0
        lax.fori_loop(0, W // COARSE, start, 0)

        def start_own(q, _):
            f = local(clin, (outer + W) // COARSE + q)
            for r in range(COARSE):
                for c in range(4):
                    for t in range(4):
                        at = 1 + W + COARSE * q + r
                        u[0, at, c, rows(t)] = u[0, at, c, rows(t)] + f
            return 0
        lax.fori_loop(0, half // COARSE, start_own, 0)
        mirror()
        solve_inner()
        share(m2, m2_ss, m2_rs, 1)

        drain(m1, m1_ss, m1_rs, 0)
        collect(m1, m1_ss, m1_rs, [0])
        w1[n - 1] = whole(m1, n) + dl[...]
        dl[...] = jnp.zeros(c_shape, F32)
        for d in range(n_count - 1, 0, -1):
            collect(m2, m2_ss, m2_rs, [d])

            @pl.when(n - d >= 1)
            def _(d=d):
                e = dl[...]
                dl[...] = c_jacobi(e * c_inv, e) + (whole(m2, n - d) - w1[n - d])
        drain(m2, m2_ss, m2_rs, 1)
        e = dl[...]
        to_line(clin, c_jacobi(e * c_inv, e))

    @pl.when(jnp.logical_not(has_prev))
    def _():
        to_line(clin, jnp.zeros(c_shape, F32))

    def finish(q, _):
        parts = []
        f = local(clin, (outer + W) // COARSE + q // 2)
        for r in range(2):
            tiles = [[u[0, 1 + W + 2 * q + r, c, rows(t)] + f for c in range(4)] for t in range(4)]
            for side in range(2):
                for t in range(4):
                    row = []
                    for e in range(zs):
                        x, y = tiles[t][2 * e], tiles[t][2 * e + 1]
                        row.append(jnp.where(h0, x, swap(y)) if side == 0 else jnp.where(h0, swap(x), y))
                    parts.append(jnp.concatenate(row, 1))
        moved = permute(jnp.concatenate(parts, 0), from_tiles)
        for r in range(2):
            for side, plane in enumerate((2 * q + r, planes - 1 - 2 * q - r)):
                for t in range(4):
                    at = (r * 8 + side * 4 + t) * cy
                    for c in range(zs):
                        raw[c, plane, pl.ds(t, cy, stride=4), :] = moved[at:at + cy, c * lanes:(c + 1) * lanes]
        return 0
    lax.fori_loop(0, half // 2, finish, 0)
    stores = [pltpu.make_async_copy(raw.at[c], out.at[0, :, :, pl.ds(c * lanes, lanes)], in_sem.at[c])
              for c in range(zs)]
    for store in stores:
        store.start()

    for cond, copy in spreads:
        @pl.when(cond)
        def _(copy=copy):
            copy.wait_send()
    for slot in (1, 2):
        @pl.when((n == 1) & there[slot])
        def _(slot=slot):
            passed[slot - 1].wait_send()

    for store in stores:
        store.wait()


def solution(mesh):
    n_count, s_count = mesh.shape["tm"], mesh.shape["space"]

    def on_device(init, labels, rates, heat):
        planes, ny, nz = init.shape
        bx, cy, cz = labels.shape
        cx = bx * s_count
        lanes = 2 * cz
        zs = nz // lanes
        half, bh, cq = planes // 2, bx // 2, cx // 2
        pad = 2 * W // COARSE
        inner, every = W + half, 2 * W + half
        dma = pltpu.SemaphoreType.DMA

        def vm(*shape):
            return pltpu.VMEM(shape, F32)

        return pl.pallas_call(
            functools.partial(kernel, n_count, s_count),
            out_shape=jax.ShapeDtypeStruct((1, planes, ny, nz), F32),
            in_specs=[pl.BlockSpec(memory_space=pl.ANY)] * 4,
            out_specs=pl.BlockSpec(memory_space=pl.ANY),
            scratch_shapes=[
                vm(zs, planes, ny, lanes), pltpu.VMEM(labels.shape, labels.dtype),
                pltpu.SMEM((1, rates.shape[0]), F32), pltpu.SMEM(heat.shape, F32),
                dma((3 + zs,)),
                vm(half, 4, 4 * cy, lanes), vm(4, half, 4, 4 * cy, lanes),
                vm(s_count, 2 * bh, cy, lanes),
                vm(n_count, s_count, bh, cy, lanes), vm(n_count, s_count, bh, cy, lanes),
                vm(n_count, cq, cy, lanes), vm(n_count, cq, cy, lanes), vm(cq, cy, lanes),
                vm(cx + 2 * pad, cy, lanes), vm(cx + 2 * pad, cy, lanes),
                vm(every, cy, lanes), vm(every // COARSE, cy, lanes), vm(every // COARSE, cy, lanes),
                vm(2, inner + 2, 4, ROWS, lanes),
                vm(W + 1, W + 2, 4, ROWS, lanes),
                vm(2, every, 4, 4 * cy, lanes),
                dma((s_count,)), dma((s_count,)),
                dma((8,)), dma((4,)),
                dma((n_count, s_count)), dma((n_count, s_count)),
                dma((n_count, s_count)), dma((n_count, s_count)),
            ],
            compiler_params=pltpu.CompilerParams(
                collective_id=0, has_side_effects=True, vmem_limit_bytes=67_043_328),
            name="parareal",
        )(init, labels, rates.reshape(1, -1), heat)

    return jax.shard_map(
        on_device,
        mesh=mesh,
        in_specs=(P("space", None, None), P("space", None, None), P(), P()),
        out_specs=P("tm", "space", None, None),
        check_vma=False,
    )
```
